32 devices in a mesh: dp: 8 (over z, y), seq: 4 (over x, core).
Axes of the slice: x: 2, y: 2, z: 4, core: 2. Of those that a mesh axis runs over, the one named last changes fastest.
Arguments:
- hidden_in: bfloat16 [16, 2048, 768], P('dp', 'seq'), may hold values from -6 to 6
- seg_lengths: int32 [16, 16], P('dp'), may hold values from 1 to 1024, 2048 in all within a row
- query_weight: bfloat16 [768, 768], replicated, may hold values from -0.3125 to 0.3125
- query_bias: float32 [768], replicated, may hold values from -3 to 3
- key_weight: bfloat16 [768, 768], replicated, may hold values from -0.21875 to 0.21875
- value_weight: bfloat16 [768, 768], replicated, may hold values from -0.21875 to 0.21875
- value_bias: float32 [768], replicated, may hold values from -3 to 3
- out_weight: bfloat16 [768, 768], replicated, may hold values from -0.875 to 0.875
- out_bias: float32 [768], replicated, may hold values from -3 to 3
- first_gain: float32 [768], replicated, may hold values from 0.5 to 1.5
- first_shift: float32 [768], replicated, may hold values from -2 to 2
- up_weight: bfloat16 [768, 3072], replicated, may hold values from -0.21875 to 0.21875
- up_bias: float32 [3072], replicated, may hold values from -3 to 3
- down_weight: bfloat16 [3072, 768], replicated, may hold values from -0.15625 to 0.15625
- down_bias: float32 [768], replicated, may hold values from -3 to 3
- second_gain: float32 [768], replicated, may hold values from 0.5 to 1.5
- second_shift: float32 [768], replicated, may hold values from -2 to 2
- cot_out: bfloat16 [16, 2048, 768], P('dp', 'seq'), may hold values from -6 to 6
- cot_pool: float32 [16, 15, 768], P('dp'), may hold values from -15 to 15
Outputs:
- layer_out: bfloat16 [16, 2048, 768], P('dp', 'seq')
- pooled: float32 [16, 15, 768], P('dp')
- grad_hidden: float32 [16, 2048, 768], P('dp', 'seq')
- grad_query_weight: float32 [768, 768], replicated
- grad_query_bias: float32 [768], replicated
- grad_key_weight: float32 [768, 768], replicated
- grad_value_weight: float32 [768, 768], replicated
- grad_value_bias: float32 [768], replicated
- grad_out_weight: float32 [768, 768], replicated
- grad_out_bias: float32 [768], replicated
- grad_first_gain: float32 [768], replicated
- grad_first_shift: float32 [768], replicated
- grad_up_weight: float32 [768, 3072], replicated
- grad_up_bias: float32 [3072], replicated
- grad_down_weight: float32 [3072, 768], replicated
- grad_down_bias: float32 [768], replicated
- grad_second_gain: float32 [768], replicated
- grad_second_shift: float32 [768], replicated
The draws below stay inside these ranges and needn't reach their ends.
Inputs may be any that keep to these rules, and one draw needn't show every extreme that they name: `seg_lengths`: a row's 16 entries add up to 2048; the last one is the row's padding; in every row some entry equals 1024.
All inputs are finite; a program needn't handle non-finite values.
Results may differ from the reference program's by a relative error of at most 0.015.
Values may be sent and summed in bfloat16 or wider, within the bound.
No kernel may reach another device: no remote copies, remote signals or barrier semaphores. Data moves between devices by JAX's collectives and lax.ppermute only.
A program may use at most 448 MiB of HBM per device.

```python
import math
import jax
import jax.numpy as jnp
import numpy as np
from jax import lax

D = 768
H = 12
HD = 64
FF = 3072
SEQ_LEN = 2048
NSENT = 15
SLOTS = 16
ROWS = 16


def steps_of(key, shape, pieces, smallest, high):
    factor_of, own = 1.0, jax.random.fold_in(key, 6)
    for dim, blocks in pieces:
        steps = jnp.exp(jax.random.uniform(jax.random.fold_in(own, dim), (blocks,), jnp.float32, smallest / len(pieces), high / len(pieces)))
        factor_of = factor_of * jnp.repeat(steps, shape[dim] // blocks).reshape([-1 if axis == dim else 1 for axis in range(len(shape))])
    return factor_of


def length_profile(count, total, most, skew):
    portions = [(1 << 20) // math.isqrt(grade ** skew) + 1 for grade in range(2, count + 1)]
    spare, holding = total - most - (count - 1), [1] * (count - 1)
    while spare > 0:
        free = [i for i in range(count - 1) if holding[i] < most]
        mass, remaining = sum([portions[i] for i in free]), spare
        for i in free:
            more = min(most - holding[i], max(1, remaining * portions[i] // mass), spare)
            holding[i] = holding[i] + more
            spare = spare - more
    return np.array([most] + holding)


def ragged(rng, amount, total, reach, skew):
    if amount == 2:
        one = jax.random.randint(rng, (), max(1, total - reach), min(reach, total - 1) + 1)
        return jnp.stack([one, total - one])
    lengths = jnp.asarray(length_profile(amount, total, reach, skew), jnp.int32)
    pairs = (amount - 1) // 2
    giver, receiver = lengths[1:1 + 2 * pairs:2], lengths[2:2 + 2 * pairs:2]
    slack = jnp.minimum(giver - 1, reach - receiver)
    passed = jax.random.randint(jax.random.fold_in(rng, 1), (pairs,), 0, 1 << 20) % (slack + 1)
    lengths = lengths.at[1:1 + 2 * pairs:2].set(giver - passed).at[2:2 + 2 * pairs:2].set(receiver + passed)
    return lengths[jax.random.permutation(jax.random.fold_in(rng, 2), amount)]


def noise(own_key, dims, scale, bound, split=(), kind=jnp.bfloat16):
    entries = scale * jax.random.normal(own_key, dims, jnp.float32)
    if split:
        entries = entries * steps_of(own_key, dims, split, -0.22, 0.18)
    return jnp.clip(entries, -bound, bound).astype(kind)


def setup_inputs(seed: int = 0) -> dict:
    streams_of = jax.random.split(jax.random.key(seed), 20)
    return {
        "hidden_in": noise(streams_of[0], (ROWS, SEQ_LEN, D), 1.0, 6.0, ((0, 8), (1, 4))),
        "seg_lengths": jax.vmap(lambda own: ragged(own, SLOTS, SEQ_LEN, SEQ_LEN // 2, 2))(jax.random.split(streams_of[1], ROWS)).reshape((ROWS, SLOTS)).astype(jnp.int32),
        "query_weight": noise(streams_of[2], (D, D), (D // 2) ** -0.5, 0.3125),
        "query_bias": noise(streams_of[3], (D,), 0.5, 3.0, (), jnp.float32),
        "key_weight": noise(streams_of[4], (D, D), D ** -0.5, 0.21875),
        "value_weight": noise(streams_of[5], (D, D), D ** -0.5, 0.21875),
        "value_bias": noise(streams_of[6], (D,), 0.5, 3.0, (), jnp.float32),
        "out_weight": noise(streams_of[7], (D, D), (D // 16) ** -0.5, 0.875),
        "out_bias": noise(streams_of[8], (D,), 0.5, 3.0, (), jnp.float32),
        "first_gain": jnp.clip(1.0 + 0.1 * jax.random.normal(streams_of[9], (D,), jnp.float32), 0.5, 1.5),
        "first_shift": noise(streams_of[10], (D,), 0.3, 2.0, (), jnp.float32),
        "up_weight": noise(streams_of[11], (D, FF), D ** -0.5, 0.21875),
        "up_bias": noise(streams_of[12], (FF,), 0.5, 3.0, (), jnp.float32),
        "down_weight": noise(streams_of[13], (FF, D), (FF // 2) ** -0.5, 0.15625),
        "down_bias": noise(streams_of[14], (D,), 0.5, 3.0, (), jnp.float32),
        "second_gain": jnp.clip(1.0 + 0.1 * jax.random.normal(streams_of[15], (D,), jnp.float32), 0.5, 1.5),
        "second_shift": noise(streams_of[16], (D,), 0.3, 2.0, (), jnp.float32),
        "cot_out": noise(streams_of[17], (ROWS, SEQ_LEN, D), 1.0, 6.0, ((0, 8), (1, 4))),
        "cot_pool": noise(streams_of[18], (ROWS, NSENT, D), 3.0, 15.0, ((0, 8),), jnp.float32),
    }


EPS = 1e-06
HIGH = lax.Precision.HIGHEST

@jax.custom_vjp
def low(v):
    return lax.optimization_barrier(v.astype(jnp.bfloat16)).astype(jnp.float32)

@jax.custom_vjp
def low_back(v):
    return v

def low_keep(v):
    return (low(v), None)

def low_pass(kept, grad):
    return (grad,)

def back_keep(v):
    return (v, None)

def back_low(kept, grad):
    return (low(grad),)
low.defvjp(low_keep, low_pass)
low_back.defvjp(back_keep, back_low)

def layer_norm(hidden, norm_gain, norm_shift):
    centred = hidden - lax.optimization_barrier(jnp.mean(hidden, axis=-1, keepdims=True))
    spread = lax.optimization_barrier(jnp.mean(centred * centred, axis=-1, keepdims=True))
    return centred * lax.rsqrt(spread + EPS) * norm_gain + norm_shift

def matmul(left, right):
    return jnp.dot(left, right, precision=HIGH, preferred_element_type=jnp.float32)

def one_row(params, row_input, segment_ends, sentence_sizes):
    w_query, b_query, w_key, w_value, b_value, w_out, b_out, gain_one, shift_one, w_up, b_up, w_down, b_down, gain_two, shift_two = params
    places = jnp.arange(SEQ_LEN, dtype=jnp.int32)
    segment = lax.optimization_barrier(jnp.sum((places[:, None] >= segment_ends[None, :]).astype(jnp.int32), axis=1)).astype(jnp.int32)
    query_heads = low_back(low(matmul(row_input, w_query) + b_query)).reshape(SEQ_LEN, H, HD)
    key_heads = low_back(low(matmul(row_input, w_key))).reshape(SEQ_LEN, H, HD)
    value_heads = low_back(low(matmul(row_input, w_value) + b_value)).reshape(SEQ_LEN, H, HD)
    scores = jnp.einsum('qhd,khd->hqk', query_heads, key_heads, precision=HIGH) * 0.125
    same_segment = segment[:, None] == segment[None, :]
    scores = low_back(jnp.where(same_segment[None], scores, -1e+30))
    probs_low = low(jax.nn.softmax(scores, axis=-1))
    attended = jnp.einsum('hqk,khd->qhd', probs_low, value_heads, precision=HIGH).reshape(SEQ_LEN, D)
    attended = low_back(low(attended))
    first_sum = row_input + low_back(matmul(attended, w_out) + b_out)
    normed = layer_norm(first_sum, gain_one, shift_one)
    pre_act = low_back(matmul(low(normed), w_up) + b_up)
    activated = low(jax.nn.gelu(pre_act, approximate=False))
    second_sum = normed + low_back(matmul(activated, w_down) + b_down)
    final_norm = layer_norm(second_sum, gain_two, shift_two)
    membership = (segment[:, None] == jnp.arange(NSENT, dtype=jnp.int32)[None, :]).astype(jnp.float32)
    pooled = matmul(membership.T, final_norm) / sentence_sizes[:, None]
    return (final_norm, pooled)

def reference(hidden_in, seg_lengths, query_weight, query_bias, key_weight, value_weight, value_bias, out_weight, out_bias, first_gain, first_shift, up_weight, up_bias, down_weight, down_bias, second_gain, second_shift, cot_out, cot_pool):
    segment_ends = jnp.cumsum(seg_lengths, axis=1).astype(jnp.int32)
    sentence_sizes = seg_lengths[:, :NSENT].astype(jnp.float32)
    params = (query_weight.astype(jnp.float32), query_bias.astype(jnp.float32), key_weight.astype(jnp.float32), value_weight.astype(jnp.float32), value_bias.astype(jnp.float32), out_weight.astype(jnp.float32), out_bias.astype(jnp.float32), first_gain.astype(jnp.float32), first_shift.astype(jnp.float32), up_weight.astype(jnp.float32), up_bias.astype(jnp.float32), down_weight.astype(jnp.float32), down_bias.astype(jnp.float32), second_gain.astype(jnp.float32), second_shift.astype(jnp.float32))

    def forward(weights, inputs):

        def row_fn(row_items):
            return jax.checkpoint(one_row)(weights, row_items[0], row_items[1], row_items[2])
        return lax.map(row_fn, (inputs, segment_ends, sentence_sizes))
    inputs = hidden_in.astype(jnp.float32)
    (final_norm, pooled), pullback = jax.vjp(forward, params, inputs)
    weight_grads, grad_hidden = pullback((cot_out.astype(jnp.float32), cot_pool.astype(jnp.float32)))
    g_query_w, g_query_b, g_key_w, g_value_w, g_value_b, g_out_w, g_out_b, g_gain_one, g_shift_one, g_up_w, g_up_b, g_down_w, g_down_b, g_gain_two, g_shift_two = weight_grads
    return (final_norm.astype(jnp.bfloat16), pooled, grad_hidden, g_query_w, g_query_b, g_key_w, g_value_w, g_value_b, g_out_w, g_out_b, g_gain_one, g_shift_one, g_up_w, g_up_b, g_down_w, g_down_b, g_gain_two, g_shift_two)
```

```python
import functools

import jax
import jax.numpy as jnp
from jax import lax
from jax.experimental import pallas as pl
from jax.experimental.pallas import tpu as pltpu
from jax.sharding import PartitionSpec as P

HD = 64
NSENT = 15
SLOTS = 16
EPS = 1e-06
HIGH = lax.Precision.HIGHEST
PAIR = 2 * HD
QB = 128
KB = 256
MASKED = -1e30
BF16 = jnp.bfloat16
F32 = jnp.float32


def swap(value, axis, bit):
    size = lax.axis_size(axis)
    return lax.ppermute(value, axis, [(i, i ^ bit) for i in range(size)])


def bit_of(axis, bit):
    return (lax.axis_index(axis) // bit) % 2


def dot(left, right, contract):
    return lax.dot_general(left, right, (contract, ((), ())), preferred_element_type=F32)


def qkv_kernel(place_ref, a_ref, b_ref, c_ref, d_ref, weight_ref, bias_ref, scale_ref, x_ref, out_ref):
    step = pl.program_id(0)
    for slot, source in enumerate((a_ref, b_ref, c_ref, d_ref)):

        @pl.when(step == slot)
        def _(source=source):
            x_ref[...] = source[...]
            total = dot(source[...], weight_ref[...], ((1,), (0,)))
            out_ref[...] = ((total + bias_ref[...]) * scale_ref[...]).astype(BF16)


def qkv(places, chunks, weight, bias, scale):
    length, width = chunks[0].shape
    columns = weight.shape[1]
    whole = lambda i, places: (0, 0)
    placed = lambda i, places: (places[i], 0)
    return pl.pallas_call(
        qkv_kernel,
        grid_spec=pltpu.PrefetchScalarGridSpec(
            num_scalar_prefetch=1,
            grid=(4,),
            in_specs=[pl.BlockSpec((length, width), whole)] * 4
            + [
                pl.BlockSpec((width, columns), whole),
                pl.BlockSpec((1, columns), whole),
                pl.BlockSpec((1, columns), whole),
            ],
            out_specs=[
                pl.BlockSpec((length, width), placed),
                pl.BlockSpec((length, columns), placed),
            ],
        ),
        out_shape=[
            jax.ShapeDtypeStruct((4 * length, width), BF16),
            jax.ShapeDtypeStruct((4 * length, columns), BF16),
        ],
        cost_estimate=pl.CostEstimate(
            flops=8 * length * width * columns, bytes_accessed=20 * length * width, transcendentals=0
        ),
    )(places, *chunks, weight, bias, scale)


def halves(block):
    lane = lax.broadcasted_iota(jnp.int32, block.shape, 1)
    zero = jnp.zeros_like(block)
    return jnp.where(lane < HD, block, zero), jnp.where(lane < HD, zero, block)


def stack_heads(block, feature=None):
    first, second = halves(block)
    if feature is not None:
        first = jnp.concatenate([first, feature], axis=1)
        second = jnp.concatenate([second, feature], axis=1)
    return jnp.concatenate([first, second], axis=0)


def merge_heads(stacked):
    first, second = stacked[:QB], stacked[QB:]
    lane = lax.broadcasted_iota(jnp.int32, first.shape, 1)
    return jnp.where(lane < HD, first, second)


def attend_kernel(start_ref, count_ref, q_ref, k_ref, v_ref, qf_ref, kf_ref, out_ref, lse_ref, score_ref, acc_ref):
    @pl.loop(0, q_ref.shape[0] // QB)
    def _(block):
        rows = pl.ds(pl.multiple_of(block * QB, QB), QB)
        start = start_ref[block] * QB
        count = count_ref[block]
        stacked = stack_heads(q_ref[rows, :], qf_ref[rows, :])

        def scores(j, top):
            keys = pl.ds(pl.multiple_of(start + j * KB, QB), KB)
            side = jnp.concatenate([k_ref[keys, :], kf_ref[keys, :]], axis=1)
            score = dot(side, stacked, ((1,), (1,)))
            score_ref[pl.ds(pl.multiple_of(j * KB, KB), KB), :] = score
            return jnp.maximum(top, jnp.max(score.reshape(KB // 8, 8, 2 * QB), axis=0))

        top = lax.fori_loop(0, count, scores, jnp.full((8, 2 * QB), -jnp.inf, F32))
        top = jnp.max(top, axis=0, keepdims=True)
        acc_ref[...] = jnp.zeros_like(acc_ref)

        def weigh(j, total):
            keys = pl.ds(pl.multiple_of(start + j * KB, QB), KB)
            soft = jnp.exp(score_ref[pl.ds(pl.multiple_of(j * KB, KB), KB), :] - top)
            value = v_ref[keys, :]
            side = jnp.concatenate([value, jnp.ones_like(value)], axis=1)
            acc_ref[...] += dot(soft.astype(BF16), side, ((0,), (0,)))
            return total + jnp.sum(soft.reshape(KB // 8, 8, 2 * QB), axis=0)

        total = lax.fori_loop(0, count, weigh, jnp.zeros((8, 2 * QB), F32))
        total = jnp.sum(total, axis=0, keepdims=True)
        lse_ref[0, pl.ds(block, 1), :] = top + jnp.log(total)
        acc = acc_ref[...]
        out_ref[rows, :] = merge_heads(acc[:, :PAIR] / acc[:, PAIR:]).astype(BF16)


def attend(starts, counts, packed, query_feature, key_feature):
    length = packed.shape[0]
    pairs = packed.shape[1] // (3 * PAIR)
    column = lambda offset: pl.BlockSpec((length, PAIR), lambda g, s, c: (0, g + offset * pairs))
    feature = pl.BlockSpec((length, PAIR), lambda g, s, c: (0, 0))
    return pl.pallas_call(
        attend_kernel,
        grid_spec=pltpu.PrefetchScalarGridSpec(
            num_scalar_prefetch=2,
            grid=(pairs,),
            in_specs=[column(0), column(1), column(2), feature, feature],
            out_specs=[
                pl.BlockSpec((length, PAIR), lambda g, s, c: (0, g)),
                pl.BlockSpec((1, length // QB, 2 * QB), lambda g, s, c: (g, 0, 0)),
            ],
            scratch_shapes=[pltpu.VMEM((length, 2 * QB), F32), pltpu.VMEM((2 * QB, 2 * PAIR), F32)],
        ),
        out_shape=[
            jax.ShapeDtypeStruct((length, pairs * PAIR), BF16),
            jax.ShapeDtypeStruct((pairs, length // QB, 2 * QB), F32),
        ],
        compiler_params=pltpu.CompilerParams(vmem_limit_bytes=48 << 20),
        cost_estimate=pl.CostEstimate(
            flops=16 * length * length * PAIR, bytes_accessed=12 * length * PAIR, transcendentals=length * length
        ),
    )(starts, counts, packed, packed, packed, query_feature, key_feature)


def attend_back_kernel(
    start_ref, count_ref, q_ref, k_ref, v_ref, o_ref, do_ref, lse_ref, qf_ref, kf_ref,
    dq_ref, dk_ref, dv_ref, dq_acc, dk_acc, dv_acc,
):
    dk_acc[...] = jnp.zeros_like(dk_acc)
    dv_acc[...] = jnp.zeros_like(dv_acc)

    @pl.loop(0, q_ref.shape[0] // QB)
    def _(block):
        rows = pl.ds(pl.multiple_of(block * QB, QB), QB)
        start = start_ref[block] * QB
        count = count_ref[block]
        query = q_ref[rows, :]
        stacked = stack_heads(query, qf_ref[rows, :])
        queries = stack_heads(query)
        upstream = do_ref[rows, :]
        ups = stack_heads(upstream)
        product = (upstream.astype(F32) * o_ref[rows, :].astype(F32)).T
        delta = jnp.concatenate(
            [jnp.sum(product[:HD], axis=0, keepdims=True), jnp.sum(product[HD:], axis=0, keepdims=True)], axis=1
        )
        lse = lse_ref[0, pl.ds(block, 1), :]
        dq_acc[...] = jnp.zeros_like(dq_acc)

        @pl.loop(0, count)
        def _(j):
            keys = pl.ds(pl.multiple_of(start + j * KB, QB), KB)
            key = k_ref[keys, :]
            score = dot(jnp.concatenate([key, kf_ref[keys, :]], axis=1), stacked, ((1,), (1,)))
            soft = jnp.exp(score - lse)
            d_soft = dot(v_ref[keys, :], ups, ((1,), (1,)))
            d_score = (soft * (d_soft - delta)).astype(BF16)
            dv_acc[keys, :] += dot(soft.astype(BF16), ups, ((1,), (0,)))
            dk_acc[keys, :] += dot(d_score, queries, ((1,), (0,)))
            dq_acc[...] += dot(d_score, key, ((0,), (0,)))

        dq_ref[rows, :] = (merge_heads(dq_acc[...]) * 0.125).astype(BF16)

    dk_ref[...] = dk_acc[...].astype(BF16)
    dv_ref[...] = dv_acc[...].astype(BF16)


def attend_back(starts, counts, packed, attended, upstream, lse, query_feature, key_feature):
    length = packed.shape[0]
    pairs = packed.shape[1] // (3 * PAIR)
    column = lambda offset: pl.BlockSpec((length, PAIR), lambda g, s, c: (0, g + offset * pairs))
    feature = pl.BlockSpec((length, PAIR), lambda g, s, c: (0, 0))
    return pl.pallas_call(
        attend_back_kernel,
        grid_spec=pltpu.PrefetchScalarGridSpec(
            num_scalar_prefetch=2,
            grid=(pairs,),
            in_specs=[column(0), column(1), column(2), column(0), column(0)]
            + [pl.BlockSpec((1, length // QB, 2 * QB), lambda g, s, c: (g, 0, 0)), feature, feature],
            out_specs=[column(0)] * 3,
            scratch_shapes=[
                pltpu.VMEM((2 * QB, PAIR), F32),
                pltpu.VMEM((length, PAIR), F32),
                pltpu.VMEM((length, PAIR), F32),
            ],
        ),
        out_shape=[jax.ShapeDtypeStruct((length, pairs * PAIR), BF16)] * 3,
        compiler_params=pltpu.CompilerParams(vmem_limit_bytes=48 << 20),
        cost_estimate=pl.CostEstimate(
            flops=40 * length * length * PAIR, bytes_accessed=20 * length * PAIR, transcendentals=length * length
        ),
    )(starts, counts, packed, packed, packed, attended, upstream, lse, query_feature, key_feature)


def reduce_step(value, axis, bit):
    half = value.shape[0] // 2
    mine = bit_of(axis, bit)
    keep = lax.dynamic_slice_in_dim(value, mine * half, half, 0)
    send = lax.dynamic_slice_in_dim(value, (1 - mine) * half, half, 0)
    got = swap(send, axis, bit)
    return (keep.astype(F32) + got.astype(F32)).astype(BF16)


def gather_step(value, axis, bit):
    got = swap(value, axis, bit)
    first = bit_of(axis, bit) == 0
    return jnp.concatenate([jnp.where(first, value, got), jnp.where(first, got, value)], axis=0)


def all_reduce(value, order):
    for axis, bit in order:
        value = reduce_step(value, axis, bit)
    for axis, bit in reversed(order):
        value = gather_step(value, axis, bit)
    return value


def sum_all(value, order):
    for axis, bit in order:
        value = value + swap(value, axis, bit)
    return value


def layer_norm(hidden, norm_gain, norm_shift):
    centred = hidden - jnp.mean(hidden, axis=-1, keepdims=True)
    spread = jnp.mean(centred * centred, axis=-1, keepdims=True)
    return centred * lax.rsqrt(spread + EPS) * norm_gain + norm_shift


def gelu_exact(values):
    return jax.nn.gelu(values, approximate=False)


def local(
    hidden_in,
    seg_lengths,
    query_weight,
    query_bias,
    key_weight,
    value_weight,
    value_bias,
    out_weight,
    out_bias,
    first_gain,
    first_shift,
    up_weight,
    up_bias,
    down_weight,
    down_bias,
    second_gain,
    second_shift,
    cot_out,
    cot_pool,
):
    _, chunk, width = hidden_in.shape
    length = 4 * chunk
    half = width // 2
    dp_bits = [1 << i for i in range((lax.axis_size("dp") - 1).bit_length())]
    dp_order = [("dp", b) for b in dp_bits]
    far, near = ("seq", 2), ("seq", 1)
    high, low = bit_of(*far), bit_of(*near)
    mine = lax.axis_index("seq")

    pick = lambda array, i: lax.dynamic_index_in_dim(array, i, 0, keepdims=False)
    own = pick(hidden_in, high)
    came = swap(pick(hidden_in, 1 - high), *far)
    own_there = swap(own, *near)
    came_there = swap(came, *near)
    cot_own = pick(cot_out, high)
    cot_came = swap(pick(cot_out, 1 - high), *far)

    lengths = pick(seg_lengths, high)
    ends = jnp.cumsum(lengths)
    begins = ends - lengths
    sizes = lengths[:NSENT].astype(F32)
    positions = jnp.arange(length, dtype=jnp.int32)
    member = (positions[:, None] >= begins[None, :]) & (positions[:, None] < ends[None, :])
    member = jnp.pad(member, ((0, 0), (0, PAIR - SLOTS)))
    query_feature = member.astype(BF16)
    key_feature = jnp.where(member, 0.0, MASKED).astype(BF16)
    block_first = jnp.arange(length // QB, dtype=jnp.int32) * QB
    block_last = block_first + QB - 1
    holds = lambda t: (t[:, None] >= begins[None, :]) & (t[:, None] < ends[None, :])
    lowest = jnp.sum(jnp.where(holds(block_first), begins[None, :], 0), axis=1)
    highest = jnp.sum(jnp.where(holds(block_last), ends[None, :], 0), axis=1)
    starts = lowest // QB
    stops = (highest + QB - 1) // QB
    counts = (stops - starts + 1) // (KB // QB)
    starts = jnp.minimum(starts, length // QB - counts * (KB // QB))

    take = lambda weight: lax.dynamic_slice_in_dim(weight, low * half, half, 1)
    packed_weight = jnp.concatenate([take(query_weight), take(key_weight), take(value_weight)], axis=1)
    vector = lambda bias: lax.dynamic_slice_in_dim(bias, low * half, half, 0)
    packed_bias = jnp.concatenate([vector(query_bias), jnp.zeros((half,), F32), vector(value_bias)])[None, :]
    scale = jnp.concatenate([jnp.full((half,), 0.125, F32), jnp.ones((2 * half,), F32)])[None, :]

    places = jnp.stack([mine, mine ^ 2, mine ^ 1, mine ^ 3]).astype(jnp.int32)
    row_input, packed = qkv(places, (own, came, own_there, came_there), packed_weight, packed_bias, scale)
    attended_heads, lse = attend(starts, counts, packed, query_feature, key_feature)

    def to_tokens(array):
        view = array.reshape(2, 2, chunk, half)
        keep = lax.dynamic_index_in_dim(view, low, 1, keepdims=False)
        send = lax.dynamic_index_in_dim(view, 1 - low, 1, keepdims=False)
        return keep.reshape(2 * chunk, half), swap(send.reshape(2 * chunk, half), *near)

    att_mine, att_other = to_tokens(attended_heads)
    out_mine = lax.dynamic_slice_in_dim(out_weight, low * half, half, 0)
    out_other = lax.dynamic_slice_in_dim(out_weight, (1 - low) * half, half, 0)

    by_place = lambda a, b: jnp.concatenate([jnp.where(high == 0, a, b), jnp.where(high == 0, b, a)], axis=0)
    inputs = by_place(own, came)
    cot = by_place(cot_own, cot_came)
    token_member = lax.dynamic_index_in_dim(member.reshape(2, 2, chunk, PAIR), low, 1, keepdims=False)
    token_member = token_member.reshape(2 * chunk, PAIR)[:, :NSENT].astype(F32)

    project = lambda a, w: dot(a, w, ((1,), (0,)))
    project_back = lambda a, w: dot(a, w, ((1,), (1,)))
    weight_grad = lambda a, g: dot(a, g, ((0,), (0,))).astype(BF16)
    column_sum = lambda g: jnp.sum(g.astype(F32), axis=0)

    first_sum = inputs.astype(F32) + project(att_mine, out_mine) + project(att_other, out_other) + out_bias
    normed, first_back = jax.vjp(layer_norm, first_sum, first_gain, first_shift)
    normed_low = normed.astype(BF16)
    pre_act = project(normed_low, up_weight) + up_bias
    activated, gelu_back = jax.vjp(gelu_exact, pre_act)
    activated_low = activated.astype(BF16)
    second_sum = normed + project(activated_low, down_weight) + down_bias
    final_norm, second_back = jax.vjp(layer_norm, second_sum, second_gain, second_shift)
    final_low = final_norm.astype(BF16)
    pool_part = lax.dot_general(
        token_member, final_norm, (((0,), (0,)), ((), ())), precision=HIGH, preferred_element_type=F32
    )
    pool_weights = pick(cot_pool, high) / sizes[:, None]
    upstream = cot.astype(F32) + jnp.dot(token_member, pool_weights, precision=HIGH, preferred_element_type=F32)
    d_second, d_gain_two, d_shift_two = second_back(upstream)
    d_branch = d_second.astype(BF16)
    d_down = weight_grad(activated_low, d_branch)
    (d_pre,) = gelu_back(project_back(d_branch, down_weight))
    d_pre_low = d_pre.astype(BF16)
    d_up = weight_grad(normed_low, d_pre_low)
    d_normed = d_second + project_back(d_pre_low, up_weight)
    d_first, d_gain_one, d_shift_one = first_back(d_normed)
    d_attn_out = d_first.astype(BF16)
    d_att_mine = project_back(d_attn_out, out_mine).astype(BF16)
    d_att_other = project_back(d_attn_out, out_other).astype(BF16)
    d_out_mine = dot(att_mine, d_attn_out, ((0,), (0,)))
    d_out_other = weight_grad(att_other, d_attn_out)

    d_att_came = swap(d_att_other, *near)
    pieces = (d_att_mine.reshape(2, 1, chunk, half), d_att_came.reshape(2, 1, chunk, half))
    d_attended = jnp.concatenate(
        [jnp.where(low == 0, pieces[0], pieces[1]), jnp.where(low == 0, pieces[1], pieces[0])], axis=1
    ).reshape(length, half)
    d_query, d_keys, d_values = attend_back(
        starts, counts, packed, attended_heads, d_attended, lse, query_feature, key_feature
    )
    d_packed = jnp.concatenate([d_query, d_keys, d_values], axis=1)
    d_hidden = project_back(d_packed, packed_weight).reshape(2, 2, chunk, width)
    d_hidden_keep = lax.dynamic_index_in_dim(d_hidden, low, 1, keepdims=False)
    d_hidden_send = lax.dynamic_index_in_dim(d_hidden, 1 - low, 1, keepdims=False)
    d_hidden_got = swap(d_hidden_send.astype(BF16), *near)
    d_inputs = d_first.reshape(2, chunk, width) + d_hidden_keep + d_hidden_got.astype(F32)
    d_packed_weight = weight_grad(row_input, d_packed)

    def to_rows(array):
        keep = pick(array, high)
        came = swap(pick(array, 1 - high), *far)
        return jnp.stack([jnp.where(high == 0, keep, came), jnp.where(high == 0, came, keep)])

    layer_out = to_rows(final_low.reshape(2, chunk, width))
    grad_own = pick(d_inputs, high)
    grad_came = swap(pick(d_inputs, 1 - high).astype(BF16), *far).astype(F32)
    grad_hidden = jnp.stack([jnp.where(high == 0, grad_own, grad_came), jnp.where(high == 0, grad_came, grad_own)])

    pool_row = (pool_part + swap(pool_part, *near)) / sizes[:, None]
    pool_far = swap(pool_row, *far)
    pooled = jnp.stack([jnp.where(high == 0, pool_row, pool_far), jnp.where(high == 0, pool_far, pool_row)])

    order_a = [far] + dp_order
    order_b = dp_order + [far]

    def reduce_columns(value):
        middle = value.shape[1] // 2
        return jnp.concatenate(
            [all_reduce(value[:, :middle], order_a), all_reduce(value[:, middle:], order_b)], axis=1
        )

    grad_down = gather_step(reduce_columns(reduce_step(d_down, *near)), *near).astype(F32)
    grad_up = gather_step(reduce_columns(reduce_step(d_up, *near)), *near).astype(F32)
    d_out = (d_out_mine + swap(d_out_other, *near).astype(F32)).astype(BF16)
    grad_out = gather_step(reduce_columns(d_out), *near).astype(F32)
    packed_all = reduce_columns(d_packed_weight)
    packed_there = swap(packed_all, *near)
    side = lambda i: jnp.concatenate(
        [
            jnp.where(low == 0, packed_all[:, i * half : (i + 1) * half], packed_there[:, i * half : (i + 1) * half]),
            jnp.where(low == 0, packed_there[:, i * half : (i + 1) * half], packed_all[:, i * half : (i + 1) * half]),
        ],
        axis=1,
    ).astype(F32)

    spread = lambda part: jnp.where(
        low == 0, jnp.concatenate([part, jnp.zeros_like(part)]), jnp.concatenate([jnp.zeros_like(part), part])
    )
    small = jnp.concatenate(
        [
            spread(column_sum(d_query)),
            spread(column_sum(d_values)),
            column_sum(d_attn_out),
            d_gain_one,
            d_shift_one,
            column_sum(d_pre_low),
            column_sum(d_branch),
            d_gain_two,
            d_shift_two,
        ]
    )
    small = sum_all(small.reshape(-1, width), [near, far] + dp_order).reshape(-1)
    hidden_units = up_weight.shape[1]
    pieces, offset = [], 0
    for size in (width, width, width, width, width, hidden_units, width, width, width):
        pieces.append(small[offset : offset + size])
        offset += size
    return (
        layer_out,
        pooled,
        grad_hidden,
        side(0),
        pieces[0],
        side(1),
        side(2),
        pieces[1],
        grad_out,
        pieces[2],
        pieces[3],
        pieces[4],
        grad_up,
        pieces[5],
        grad_down,
        pieces[6],
        pieces[7],
        pieces[8],
    )


def solution(mesh):
    tokens, rows = P("dp", "seq", None), P("dp", None)
    pool = P("dp", None, None)
    return jax.shard_map(
        local,
        mesh=mesh,
        in_specs=(tokens, rows) + (P(),) * 15 + (tokens, pool),
        out_specs=(tokens, pool, tokens) + (P(),) * 15,
        check_vma=False,
    )
```

```python
import jax
import jax.numpy as jnp
from jax import lax
from jax.experimental import pallas as pl
from jax.experimental.pallas import tpu as pltpu
from jax.sharding import PartitionSpec as P

HD = 64
NSENT = 15
SLOTS = 16
LONGEST = 1024
EPS = 1e-06
PAIR = 2 * HD
GRAIN = 128
QB = 256
KB = 256
TB = 256
MASKED = -1e30
BF16 = jnp.bfloat16
F32 = jnp.float32
NN = ((1,), (0,))
NT = ((1,), (1,))
TN = ((0,), (0,))


def swap(value, axis, bit):
    size = lax.axis_size(axis)
    return lax.ppermute(value, axis, [(i, i ^ bit) for i in range(size)])


def bit_of(axis, bit):
    return (lax.axis_index(axis) // bit) % 2


def dot(left, right, contract):
    return lax.dot_general(left, right, (contract, ((), ())), preferred_element_type=F32)


def whole(shape):
    return pl.BlockSpec(shape, lambda *_: (0,) * len(shape), pipeline_mode=pl.Buffered(1))


def params(mib):
    return pltpu.CompilerParams(vmem_limit_bytes=mib << 20)


def cost(flops, moved, exps=0):
    return pl.CostEstimate(flops=flops, bytes_accessed=moved, transcendentals=exps)


def shifted(source_ref, start, count):
    base = pl.multiple_of((start // 16) * 16, 16)
    row = lax.broadcasted_iota(jnp.int32, (count, count + GRAIN), 0)
    column = lax.broadcasted_iota(jnp.int32, (count, count + GRAIN), 1)
    select = (column == row + (start - base)).astype(BF16)
    return dot(select, source_ref[pl.ds(base, count + GRAIN), :], NN).astype(BF16)


def wrap(ref, length):
    ref[length : length + QB + GRAIN, :] = ref[: QB + GRAIN, :]


def project_kernel(info_ref, a_ref, b_ref, c_ref, d_ref, weight_ref, bias_ref, scale_ref, x_ref, out_ref, row_ref):
    step = pl.program_id(0)
    chunk = a_ref.shape[0]
    length = 4 * chunk

    @pl.when(step == 0)
    def _():
        for slot, source in enumerate((a_ref, b_ref, c_ref, d_ref)):
            row_ref[pl.ds(pl.multiple_of(info_ref[1 + slot] * chunk, chunk), chunk), :] = source[...]
        wrap(row_ref, length)

    part = shifted(row_ref, (info_ref[0] + step * QB) % length, QB)
    x_ref[...] = part
    out_ref[...] = ((dot(part, weight_ref[...], NN) + bias_ref[...]) * scale_ref[...]).astype(BF16)


def project(info, chunks, weight, bias, scale):
    chunk, width = chunks[0].shape
    columns = weight.shape[1]
    length = 4 * chunk
    return pl.pallas_call(
        project_kernel,
        grid_spec=pltpu.PrefetchScalarGridSpec(
            num_scalar_prefetch=1,
            grid=(length // QB,),
            in_specs=[whole((chunk, width))] * 4 + [whole((width, columns)), whole((1, columns)), whole((1, columns))],
            out_specs=[
                pl.BlockSpec((QB, width), lambda i, _: (i, 0)),
                pl.BlockSpec((QB, columns), lambda i, _: (i, 0)),
            ],
            scratch_shapes=[pltpu.VMEM((length + QB + GRAIN, width), BF16)],
        ),
        out_shape=[jax.ShapeDtypeStruct((length, width), BF16), jax.ShapeDtypeStruct((length, columns), BF16)],
        compiler_params=params(40),
        cost_estimate=cost(2 * length * width * (columns + QB), 14 * length * width),
        name="project",
    )(info, *chunks, weight, bias, scale)


def stack_heads(block, feature=None):
    lane = lax.broadcasted_iota(jnp.int32, block.shape, 1)
    zero = jnp.zeros_like(block)
    first, second = jnp.where(lane < HD, block, zero), jnp.where(lane < HD, zero, block)
    if feature is not None:
        first = jnp.concatenate([first, feature], axis=1)
        second = jnp.concatenate([second, feature], axis=1)
    return jnp.concatenate([first, second], axis=0)


def merge_heads(stacked):
    first, second = stacked[:QB], stacked[QB:]
    lane = lax.broadcasted_iota(jnp.int32, first.shape, 1)
    return jnp.where(lane < HD, first, second)


def fold(block, how):
    return how(block.reshape(block.shape[0] // 8, 8, block.shape[1]), axis=0)


def attend_kernel(info_ref, packed_ref, qf_ref, kf_ref, rolled_ref, keep_ref, send_ref, lse_ref, score_ref, acc_ref, row_ref):
    length = packed_ref.shape[0]
    pairs = packed_ref.shape[1] // (3 * PAIR)
    column = lambda pair, part: slice((3 * pair + part) * PAIR, (3 * pair + part + 1) * PAIR)
    lanes = lambda pair: slice(pair * PAIR, (pair + 1) * PAIR)
    stats = lambda pair: slice(pair * 2 * QB, (pair + 1) * 2 * QB)

    def weigh(pair, keys, scores, top):
        soft = jnp.exp(scores - top)
        value = packed_ref[keys, column(pair, 2)]
        side = jnp.concatenate([value, jnp.ones_like(value)], axis=1)
        return dot(soft.astype(BF16), side, TN), fold(soft, jnp.sum)

    def finish(block, rows, pair, top, total, acc):
        total = jnp.sum(total, axis=0, keepdims=True)
        lse_ref[pl.ds(block, 1), stats(pair)] = top + jnp.log(total)
        row_ref[rows, lanes(pair)] = merge_heads(acc[:, :PAIR] / acc[:, PAIR:]).astype(BF16)

    @pl.loop(0, LONGEST // QB)
    def _(block):
        rows = pl.ds(pl.multiple_of(block * QB, QB), QB)
        size = LONGEST // 2
        tops = {}

        def look(pair, k):
            stacked = stack_heads(packed_ref[rows, column(pair, 0)])
            score = dot(packed_ref[k : k + size, column(pair, 1)], stacked, NT)
            score_ref[pair, k : k + size, :] = score
            top = fold(score, jnp.max)
            tops[pair] = top if k == 0 else jnp.maximum(tops[pair], top)

        for k in (0, size):
            look(0, k)
        for pair in range(pairs):
            top = jnp.max(tops[pair], axis=0, keepdims=True)
            acc = total = None
            for k in (0, size):
                if pair + 1 < pairs:
                    look(pair + 1, k)
                more, add = weigh(pair, slice(k, k + size), score_ref[pair, k : k + size, :], top)
                acc = more if acc is None else acc + more
                total = add if total is None else total + add
            finish(block, rows, pair, top, total, acc)

    @pl.loop(LONGEST // QB, length // QB)
    def _(block):
        rows = pl.ds(pl.multiple_of(block * QB, QB), QB)
        start = info_ref[1 + block] * GRAIN
        count = info_ref[1 + length // QB + block]
        stacked = [stack_heads(packed_ref[rows, column(pair, 0)], qf_ref[rows, :]) for pair in range(pairs)]

        def look(j, tops):
            keys = pl.ds(pl.multiple_of(start + j * KB, GRAIN), KB)
            found = []
            for pair in range(pairs):
                side = jnp.concatenate([packed_ref[keys, column(pair, 1)], kf_ref[keys, :]], axis=1)
                score = dot(side, stacked[pair], NT)
                score_ref[pair, pl.ds(pl.multiple_of(j * KB, KB), KB), :] = score
                found.append(jnp.maximum(tops[pair], fold(score, jnp.max)))
            return tuple(found)

        tops = lax.fori_loop(0, count, look, (jnp.full((8, 2 * QB), -jnp.inf, F32),) * pairs)
        tops = [jnp.max(top, axis=0, keepdims=True) for top in tops]
        acc_ref[...] = jnp.zeros_like(acc_ref)

        def take(j, totals):
            keys = pl.ds(pl.multiple_of(start + j * KB, GRAIN), KB)
            found = []
            for pair in range(pairs):
                scores = score_ref[pair, pl.ds(pl.multiple_of(j * KB, KB), KB), :]
                more, add = weigh(pair, keys, scores, tops[pair])
                acc_ref[pair] += more
                found.append(totals[pair] + add)
            return tuple(found)

        totals = lax.fori_loop(0, count, take, (jnp.zeros((8, 2 * QB), F32),) * pairs)
        for pair in range(pairs):
            finish(block, rows, pair, tops[pair], totals[pair], acc_ref[pair])

    rolled_ref[...] = row_ref[:length, :]
    wrap(row_ref, length)
    chunk = length // 4
    for block in range(length // QB):
        part = shifted(row_ref, (block * QB - info_ref[0] + length) % length, QB)
        place, inside = divmod(block * QB, chunk)
        rows = slice(place // 2 * chunk + inside, place // 2 * chunk + inside + QB)
        own = info_ref[1 + 2 * (length // QB)] == place % 2

        @pl.when(own)
        def _(part=part, rows=rows):
            keep_ref[rows, :] = part

        @pl.when(jnp.logical_not(own))
        def _(part=part, rows=rows):
            send_ref[rows, :] = part


def attend(info, packed, query_feature, key_feature):
    length, columns = packed.shape
    width = columns // 3
    pairs = width // PAIR
    tokens = jax.ShapeDtypeStruct((length // 2, width), BF16)
    shapes = [
        jax.ShapeDtypeStruct((length, width), BF16),
        tokens,
        tokens,
        jax.ShapeDtypeStruct((length // QB, 2 * pairs * QB), F32),
    ]
    return pl.pallas_call(
        attend_kernel,
        grid_spec=pltpu.PrefetchScalarGridSpec(
            num_scalar_prefetch=1,
            grid=(1,),
            in_specs=[whole((length, columns)), whole((length, PAIR)), whole((length, PAIR))],
            out_specs=[whole(s.shape) for s in shapes],
            scratch_shapes=[
                pltpu.VMEM((pairs, length // 2, 2 * QB), F32),
                pltpu.VMEM((pairs, 2 * QB, 2 * PAIR), F32),
                pltpu.VMEM((length + QB + GRAIN, width), BF16),
            ],
        ),
        out_shape=shapes,
        compiler_params=params(48),
        cost_estimate=cost(6 * length * length * width, 12 * length * width, length * length),
        name="attend",
    )(info, packed, query_feature, key_feature)


def roll_back_kernel(info_ref, mine_ref, came_ref, rolled_ref, out_ref, delta_ref, row_ref):
    length, width = out_ref.shape
    chunk = length // 4
    for half in range(2):
        own = pl.multiple_of((2 * half + info_ref[1]) * chunk, chunk)
        other = pl.multiple_of((2 * half + 1 - info_ref[1]) * chunk, chunk)
        row_ref[pl.ds(own, chunk), :] = mine_ref[half * chunk : (half + 1) * chunk, :]
        row_ref[pl.ds(other, chunk), :] = came_ref[half * chunk : (half + 1) * chunk, :]
    wrap(row_ref, length)
    for block in range(length // QB):
        rows = slice(block * QB, (block + 1) * QB)
        part = shifted(row_ref, (block * QB + info_ref[0]) % length, QB)
        out_ref[rows, :] = part
        product = part.astype(F32) * rolled_ref[rows, :].astype(F32)
        for head in range(width // HD):
            if head % 2 == 0:
                turned = product[:, head * HD : head * HD + PAIR].T
            line = jnp.sum(turned[head % 2 * HD : (head % 2 + 1) * HD], axis=0, keepdims=True)
            delta_ref[block : block + 1, head * QB : (head + 1) * QB] = line


def roll_back(info, mine, came, rolled):
    length, width = rolled.shape
    shapes = [
        jax.ShapeDtypeStruct((length, width), BF16),
        jax.ShapeDtypeStruct((length // QB, width // HD * QB), F32),
    ]
    return pl.pallas_call(
        roll_back_kernel,
        grid_spec=pltpu.PrefetchScalarGridSpec(
            num_scalar_prefetch=1,
            grid=(1,),
            in_specs=[whole(mine.shape), whole(came.shape), whole(rolled.shape)],
            out_specs=[whole(s.shape) for s in shapes],
            scratch_shapes=[pltpu.VMEM((length + QB + GRAIN, width), BF16)],
        ),
        out_shape=shapes,
        compiler_params=params(32),
        cost_estimate=cost(2 * length * width * QB, 8 * length * width),
        name="roll_back",
    )(info, mine, came, rolled)


def back_step(key, side, stacked, queries, ups, value, lse, delta):
    soft = jnp.exp(dot(side, stacked, NT) - lse)
    d_soft = dot(value, ups, NT)
    d_score = (soft * (d_soft - delta)).astype(BF16)
    return dot(d_score, queries, NN), dot(soft.astype(BF16), ups, NN), dot(d_score, key, TN)


def long_back_kernel(packed_ref, up_ref, lse_ref, delta_ref, out_ref, dk_acc, dv_acc):
    dk_acc[...] = jnp.zeros_like(dk_acc)
    dv_acc[...] = jnp.zeros_like(dv_acc)
    size = LONGEST // 2

    @pl.loop(0, LONGEST // QB)
    def _(block):
        rows = pl.ds(pl.multiple_of(block * QB, QB), QB)
        queries = stack_heads(packed_ref[rows, :PAIR])
        ups = stack_heads(up_ref[rows, :])
        lse, delta = lse_ref[pl.ds(block, 1), :], delta_ref[pl.ds(block, 1), :]
        dq = None
        for k in (0, size):
            keys = slice(k, k + size)
            key = packed_ref[keys, PAIR : 2 * PAIR]
            dk, dv, more = back_step(key, key, queries, queries, ups, packed_ref[keys, 2 * PAIR :], lse, delta)
            dk_acc[keys, :] += dk
            dv_acc[keys, :] += dv
            dq = more if dq is None else dq + more
        out_ref[rows, :PAIR] = (merge_heads(dq) * 0.125).astype(BF16)

    out_ref[:, PAIR : 2 * PAIR] = dk_acc[...].astype(BF16)
    out_ref[:, 2 * PAIR :] = dv_acc[...].astype(BF16)


def long_back(pair, packed, upstream, lse, delta):
    at = lambda *shape: pl.BlockSpec(shape, lambda i: (0, pair), pipeline_mode=pl.Buffered(1))
    blocks = packed.shape[0] // QB
    return pl.pallas_call(
        long_back_kernel,
        grid=(1,),
        in_specs=[at(LONGEST, 3 * PAIR), at(LONGEST, PAIR), at(blocks, 2 * QB), at(blocks, 2 * QB)],
        out_specs=whole((LONGEST, 3 * PAIR)),
        scratch_shapes=[pltpu.VMEM((LONGEST, PAIR), F32)] * 2,
        out_shape=jax.ShapeDtypeStruct((LONGEST, 3 * PAIR), BF16),
        compiler_params=params(40),
        cost_estimate=cost(40 * LONGEST * LONGEST * PAIR, 16 * LONGEST * PAIR, LONGEST * LONGEST),
        name="long_back",
    )(packed, upstream, lse, delta)


def rest_back_kernel(info_ref, packed_ref, up_ref, lse_ref, delta_ref, qf_ref, kf_ref, out_ref, dk_acc, dv_acc, dq_acc):
    length, pairs = packed_ref.shape[0], packed_ref.shape[1] // (3 * PAIR)
    first, blocks = LONGEST // QB, (length + LONGEST) // QB
    column = lambda pair, part: slice((3 * pair + part) * PAIR, (3 * pair + part + 1) * PAIR)
    lanes = lambda pair: slice(pair * PAIR, (pair + 1) * PAIR)
    stats = lambda pair: slice(pair * 2 * QB, (pair + 1) * 2 * QB)
    dk_acc[...] = jnp.zeros_like(dk_acc)
    dv_acc[...] = jnp.zeros_like(dv_acc)

    @pl.loop(0, length // QB)
    def _(block):
        rows = pl.ds(pl.multiple_of(block * QB, QB), QB)
        start = info_ref[1 + first + block] * GRAIN - LONGEST
        count = info_ref[1 + blocks + first + block]
        feature = qf_ref[rows, :]
        ready = []
        for pair in range(pairs):
            query = packed_ref[rows, column(pair, 0)]
            line = pl.ds(first + block, 1)
            ready.append(
                (
                    stack_heads(query, feature),
                    stack_heads(query),
                    stack_heads(up_ref[rows, lanes(pair)]),
                    lse_ref[line, stats(pair)],
                    delta_ref[line, stats(pair)],
                )
            )
        dq_acc[...] = jnp.zeros_like(dq_acc)

        @pl.loop(0, count)
        def _(j):
            keys = pl.ds(pl.multiple_of(start + j * KB, GRAIN), KB)
            for pair in range(pairs):
                stacked, queries, ups, lse, delta = ready[pair]
                key = packed_ref[keys, column(pair, 1)]
                side = jnp.concatenate([key, kf_ref[keys, :]], axis=1)
                dk, dv, dq = back_step(key, side, stacked, queries, ups, packed_ref[keys, column(pair, 2)], lse, delta)
                dk_acc[keys, lanes(pair)] += dk
                dv_acc[keys, lanes(pair)] += dv
                dq_acc[pair] += dq

        for pair in range(pairs):
            out_ref[rows, column(pair, 0)] = (merge_heads(dq_acc[pair]) * 0.125).astype(BF16)

    for pair in range(pairs):
        out_ref[:, column(pair, 1)] = dk_acc[:, lanes(pair)].astype(BF16)
        out_ref[:, column(pair, 2)] = dv_acc[:, lanes(pair)].astype(BF16)


def rest_back(info, packed, upstream, lse, delta, query_feature, key_feature):
    length, columns = packed.shape
    rest, width = length - LONGEST, columns // 3
    pairs = width // PAIR
    later = lambda w: pl.BlockSpec((rest, w), lambda i, _: (1, 0), pipeline_mode=pl.Buffered(1))
    return pl.pallas_call(
        rest_back_kernel,
        grid_spec=pltpu.PrefetchScalarGridSpec(
            num_scalar_prefetch=1,
            grid=(1,),
            in_specs=[later(columns), later(width), whole(lse.shape), whole(delta.shape), later(PAIR), later(PAIR)],
            out_specs=whole((rest, columns)),
            scratch_shapes=[
                pltpu.VMEM((rest, width), F32),
                pltpu.VMEM((rest, width), F32),
                pltpu.VMEM((pairs, 2 * QB, PAIR), F32),
            ],
        ),
        out_shape=jax.ShapeDtypeStruct((rest, columns), BF16),
        compiler_params=params(40),
        cost_estimate=cost(24 * rest * rest * width, 16 * rest * width, rest * rest),
        name="rest_back",
    )(info, packed, upstream, lse, delta, query_feature, key_feature)


def input_grad_kernel(info_ref, *refs):
    pieces, rest_ref, weight_ref, keep_ref, send_ref, row_ref = refs[:-5], *refs[-5:]
    length = row_ref.shape[0] - QB - GRAIN
    width = 3 * PAIR
    for block in range(LONGEST // QB):
        rows = slice(block * QB, (block + 1) * QB)
        total = None
        for pair, piece in enumerate(pieces):
            more = dot(piece[rows, :], weight_ref[:, pair * width : (pair + 1) * width], NT)
            total = more if total is None else total + more
        row_ref[rows, :] = total.astype(BF16)
    for block in range(rest_ref.shape[0] // QB):
        rows = slice(block * QB, (block + 1) * QB)
        row_ref[LONGEST + block * QB : LONGEST + (block + 1) * QB, :] = dot(rest_ref[rows, :], weight_ref[...], NT).astype(BF16)
    wrap(row_ref, length)
    chunk = length // 4
    for block in range(length // QB):
        part = shifted(row_ref, (block * QB - info_ref[0] + length) % length, QB)
        place, inside = divmod(block * QB, chunk)
        rows = slice(place // 2 * chunk + inside, place // 2 * chunk + inside + QB)
        own = info_ref[1] == place % 2

        @pl.when(own)
        def _(part=part, rows=rows):
            keep_ref[rows, :] = part

        @pl.when(jnp.logical_not(own))
        def _(part=part, rows=rows):
            send_ref[rows, :] = part


def input_grad(info, pieces, rest, weight):
    width, columns = weight.shape
    length = LONGEST + rest.shape[0]
    tokens = jax.ShapeDtypeStruct((length // 2, width), BF16)
    return pl.pallas_call(
        input_grad_kernel,
        grid_spec=pltpu.PrefetchScalarGridSpec(
            num_scalar_prefetch=1,
            grid=(1,),
            in_specs=[whole(p.shape) for p in pieces] + [whole(rest.shape), whole(weight.shape)],
            out_specs=[whole(tokens.shape)] * 2,
            scratch_shapes=[pltpu.VMEM((length + QB + GRAIN, width), BF16)],
        ),
        out_shape=[tokens, tokens],
        compiler_params=params(40),
        cost_estimate=cost(2 * length * width * (columns + QB), 8 * length * width),
        name="input_grad",
    )(info, *pieces, rest, weight)


def gelu_both(value):
    cdf = 0.5 * lax.erf(value * 0.7071067811865476) + 0.5
    return value * cdf, cdf + value * (jnp.exp(value * value * -0.5) * 0.3989422804014327)


def normalise(value):
    centred = value - jnp.mean(value, axis=-1, keepdims=True)
    rate = lax.rsqrt(jnp.mean(centred * centred, axis=-1, keepdims=True) + EPS)
    return centred * rate, rate


def normalise_back(upstream, normal, rate, gain):
    scaled = upstream * gain
    first = jnp.mean(scaled, axis=-1, keepdims=True)
    second = jnp.mean(scaled * normal, axis=-1, keepdims=True)
    return rate * (scaled - first - normal * second)


def rows_sum(value):
    return jnp.sum(value, axis=0, keepdims=True)


def tokens_kernel(
    info_ref, mine_ref, other_ref, xa_ref, xb_ref, ca_ref, cb_ref, member_ref, pool_weight_ref,
    out_mine_ref, out_other_ref, up_ref, down_ref, vector_ref, up_bias_ref,
    out_ref, act_ref, branch_ref, normed_ref, pre_ref, attn_ref, first_ref, d_mine_ref, d_other_ref,
    pool_ref, small_ref, up_small_ref, slope_ref,
):
    step = pl.program_id(0)
    half = pl.num_programs(0) // 2

    @pl.when(step == 0)
    def _():
        pool_ref[...] = jnp.zeros_like(pool_ref)
        small_ref[...] = jnp.zeros_like(small_ref)
        up_small_ref[...] = jnp.zeros_like(up_small_ref)

    out_bias, gain_one, shift_one, down_bias, gain_two, shift_two = [vector_ref[k : k + 1, :] for k in range(6)]
    hidden = up_ref.shape[1]
    width = vector_ref.shape[1]
    own = info_ref[0] == step // half
    inputs = jnp.where(own, xa_ref[...], xb_ref[...]).astype(F32)
    first_sum = inputs + dot(mine_ref[...], out_mine_ref[...], NN) + dot(other_ref[...], out_other_ref[...], NN) + out_bias
    normal_one, rate_one = normalise(first_sum)
    normed = normal_one * gain_one + shift_one
    normed_low = normed.astype(BF16)
    normed_ref[...] = normed_low
    second_sum = normed + down_bias
    for c in range(0, hidden, width):
        cols = slice(c, c + width)
        act, slope = gelu_both(dot(normed_low, up_ref[:, cols], NN) + up_bias_ref[:, cols])
        act = act.astype(BF16)
        act_ref[:, cols] = act
        slope_ref[:, cols] = slope
        second_sum = second_sum + dot(act, down_ref[cols, :], NN)
    normal_two, rate_two = normalise(second_sum)
    final = (normal_two * gain_two + shift_two).astype(BF16)
    out_ref[...] = final
    member = member_ref[...]
    pool_ref[...] += dot(member, final, TN)[:SLOTS]
    upstream = jnp.where(own, ca_ref[...], cb_ref[...]).astype(F32)
    upstream = upstream + dot(jnp.concatenate([member, member], axis=1), pool_weight_ref[...], NN)
    d_second = normalise_back(upstream, normal_two, rate_two, gain_two)
    branch = d_second.astype(BF16)
    branch_ref[...] = branch
    d_normed = d_second
    for c in range(0, hidden, width):
        cols = slice(c, c + width)
        pre = (dot(branch, down_ref[cols, :], NT) * slope_ref[:, cols]).astype(BF16)
        pre_ref[:, cols] = pre
        up_small_ref[:, cols] += rows_sum(pre.astype(F32))
        d_normed = d_normed + dot(pre, up_ref[:, cols], NT)
    first = normalise_back(d_normed, normal_one, rate_one, gain_one)
    first_ref[...] = first
    attn = first.astype(BF16)
    attn_ref[...] = attn
    d_mine_ref[...] = dot(attn, out_mine_ref[...], NT).astype(BF16)
    d_other_ref[...] = dot(attn, out_other_ref[...], NT).astype(BF16)
    small_ref[...] += jnp.concatenate(
        [
            rows_sum(attn.astype(F32)),
            rows_sum(d_normed * normal_one),
            rows_sum(d_normed),
            rows_sum(branch.astype(F32)),
            rows_sum(upstream * normal_two),
            rows_sum(upstream),
            jnp.zeros((2, width), F32),
        ],
        axis=0,
    )


def token_layers(info, mine, other, own, came, cot_own, cot_came, member, pool_weight, out_mine, out_other, up, down, vectors, up_bias):
    count, head_width = mine.shape
    width, hidden = up.shape
    chunk = own.shape[0]
    per = chunk // TB
    token = lambda w: pl.BlockSpec((TB, w), lambda i, _: (i, 0))
    piece = pl.BlockSpec((TB, width), lambda i, _: (i % per, 0))
    placed = pl.BlockSpec((TB, PAIR), lambda i, info: (info[1 + i // per] * per + i % per, 0))
    tokens = [
        (width, BF16), (hidden, BF16), (width, BF16), (width, BF16), (hidden, BF16), (width, BF16), (width, F32),
        (head_width, BF16), (head_width, BF16),
    ]
    sums = [(SLOTS, width), (8, width), (1, hidden)]
    held = lambda shape: pl.BlockSpec(shape, lambda i, _: (0, 0))
    return pl.pallas_call(
        tokens_kernel,
        grid_spec=pltpu.PrefetchScalarGridSpec(
            num_scalar_prefetch=1,
            grid=(count // TB,),
            in_specs=[token(head_width), token(head_width), piece, piece, piece, piece, placed]
            + [whole(a.shape) for a in (pool_weight, out_mine, out_other, up, down, vectors, up_bias)],
            out_specs=[token(w) for w, _ in tokens] + [held(s) for s in sums],
            scratch_shapes=[pltpu.VMEM((TB, hidden), F32)],
        ),
        out_shape=[jax.ShapeDtypeStruct((count, w), d) for w, d in tokens] + [jax.ShapeDtypeStruct(s, F32) for s in sums],
        compiler_params=params(58),
        cost_estimate=cost(4 * count * width * (2 * hidden + width), 8 * width * hidden + 40 * count * width, 2 * count * hidden),
        name="token_layers",
    )(info, mine, other, own, came, cot_own, cot_came, member, pool_weight, out_mine, out_other, up, down, vectors, up_bias)


def product_kernel(add, info_ref, left_ref, right_ref, *refs):
    total = dot(left_ref[...], right_ref[...], TN)
    if add:
        total = total + refs[0][...].astype(F32)
    refs[-1][...] = total.astype(BF16)


def product(side, left, right, there=None):
    count, rows = left.shape
    columns = right.shape[1]
    wide = min(rows, columns)
    panels = max(rows, columns) // wide // 2
    moved = pl.BlockSpec((count, wide), lambda i, info: (0, info[0] * panels + i))
    out = pl.BlockSpec((wide, wide), lambda i, _: (i, 0))
    extra = [] if there is None else [there]
    return pl.pallas_call(
        lambda *refs: product_kernel(bool(extra), *refs),
        grid_spec=pltpu.PrefetchScalarGridSpec(
            num_scalar_prefetch=1,
            grid=(panels,),
            in_specs=[
                moved if rows > columns else whole(left.shape),
                moved if columns > rows else whole(right.shape),
            ]
            + [out] * len(extra),
            out_specs=out,
        ),
        out_shape=jax.ShapeDtypeStruct((panels * wide, wide), BF16),
        compiler_params=params(40),
        cost_estimate=cost(2 * count * panels * wide * wide, 2 * count * (panels + 1) * wide),
        name="product",
    )(side, left, right, *extra)


def head_product_kernel(add, left_ref, right_ref, *refs):
    total = dot(left_ref[...], right_ref[...], TN)
    if add:
        total = total + refs[0][...].astype(F32)
    refs[-1][...] = total.astype(BF16)


def head_product(left, right, there=None):
    extra = [] if there is None else [there]
    shape = (left.shape[1], right.shape[1])
    return pl.pallas_call(
        lambda *refs: head_product_kernel(bool(extra), *refs),
        out_shape=jax.ShapeDtypeStruct(shape, BF16),
        compiler_params=params(32),
        cost_estimate=cost(2 * left.size * right.shape[1], 4 * left.size),
        name="head_product",
    )(left, right, *extra)


def packed_product_kernel(bit_ref, x_ref, *refs):
    pairs = (len(refs) - 2) // 3
    pieces, rest_ref, outs, bias_ref = refs[:pairs], refs[pairs], refs[pairs + 1 : -1], refs[-1]
    width = 3 * PAIR
    for pair, piece in enumerate(pieces):
        columns = slice(pair * width, (pair + 1) * width)
        later = rest_ref[:, columns]
        total = dot(x_ref[:LONGEST, :], piece[...], TN) + dot(x_ref[LONGEST:, :], later, TN)
        half = total.shape[0] // 2
        upper = bit_ref[pair] == 1
        outs[2 * pair][...] = jnp.where(upper, total[half:], total[:half]).astype(BF16)
        outs[2 * pair + 1][...] = jnp.where(upper, total[:half], total[half:]).astype(BF16)
        bias_ref[:, columns] = rows_sum(piece[...].astype(F32)) + rows_sum(later.astype(F32))


def packed_product(bits, rolled, pieces, rest):
    length, width = rolled.shape
    part = jax.ShapeDtypeStruct((width // 2, 3 * PAIR), BF16)
    shapes = [part] * (2 * len(pieces)) + [jax.ShapeDtypeStruct((1, rest.shape[1]), F32)]
    return pl.pallas_call(
        packed_product_kernel,
        grid_spec=pltpu.PrefetchScalarGridSpec(
            num_scalar_prefetch=1,
            grid=(1,),
            in_specs=[whole(rolled.shape)] + [whole(p.shape) for p in pieces] + [whole(rest.shape)],
            out_specs=[whole(s.shape) for s in shapes],
        ),
        out_shape=shapes,
        compiler_params=params(40),
        cost_estimate=cost(2 * length * width * rest.shape[1], 8 * length * width),
        name="packed_product",
    )(bits, rolled, *pieces, rest)


def split_kernel(bit_ref, down_ref, up_ref, out_ref, *refs):
    cut = refs[0].shape[0] * 2
    tail = down_ref.shape[0] - cut
    head = out_ref.shape[0]
    for part, source in enumerate((down_ref, up_ref)):
        upper = bit_ref[part] == 1
        lower_half, upper_half = source[: cut // 2, :], source[cut // 2 : cut, :]
        refs[2 * part][...] = jnp.where(upper, upper_half, lower_half)
        refs[2 * part + 1][...] = jnp.where(upper, lower_half, upper_half)
    upper = bit_ref[2] == 1
    last = jnp.concatenate([down_ref[cut:, :], up_ref[cut:, :], out_ref[...]], axis=0)
    half = (2 * tail + head) // 2
    refs[4][...] = jnp.where(upper, last[half:], last[:half])
    refs[5][...] = jnp.where(upper, last[:half], last[half:])


def split(bits, down, up, out):
    third = (down.shape[0] + up.shape[0] + out.shape[0]) // 3
    shape = jax.ShapeDtypeStruct((third // 2, down.shape[1]), BF16)
    return pl.pallas_call(
        split_kernel,
        grid_spec=pltpu.PrefetchScalarGridSpec(
            num_scalar_prefetch=1,
            grid=(1,),
            in_specs=[whole(down.shape), whole(up.shape), whole(out.shape)],
            out_specs=[whole(shape.shape)] * 6,
        ),
        out_shape=[shape] * 6,
        compiler_params=params(32),
        cost_estimate=cost(3 * down.size, 12 * down.size),
        name="split",
    )(bits, down, up, out)


def combine_kernel(last, bit_ref, *refs):
    count = len(refs) // (3 if last else 4)
    for part in range(count):
        keep, got, outs = refs[2 * part], refs[2 * part + 1], refs[2 * count :]
        total = lambda rows: (keep[rows].astype(F32) + got[rows].astype(F32)).astype(BF16)
        if last:
            outs[part][...] = total(slice(None))
        else:
            half = keep.shape[0] // 2
            bit = bit_ref[part]
            outs[2 * part][...] = total(pl.ds(bit * half, half))
            outs[2 * part + 1][...] = total(pl.ds((1 - bit) * half, half))


def combine(bits, keeps, gots, last):
    operands = [a for pair in zip(keeps, gots) for a in pair]
    shapes = []
    for keep in keeps:
        n, rows, columns = keep.shape
        shapes += [jax.ShapeDtypeStruct(keep.shape, BF16)] if last else [jax.ShapeDtypeStruct((n // 2, rows, columns), BF16)] * 2
    size = sum(k.size for k in keeps)
    outs = pl.pallas_call(
        lambda *refs: combine_kernel(last, *refs),
        grid_spec=pltpu.PrefetchScalarGridSpec(
            num_scalar_prefetch=1,
            grid=(1,),
            in_specs=[whole(a.shape) for a in operands],
            out_specs=[whole(s.shape) for s in shapes],
        ),
        out_shape=shapes,
        compiler_params=params(32),
        cost_estimate=cost(2 * size, 6 * size),
        name="combine",
    )(bits, *operands)
    return (outs, None) if last else (outs[::2], outs[1::2])


def join_kernel(bit_ref, *refs):
    count = len(refs) // 3
    for part in range(count):
        mine, got, out = refs[2 * part], refs[2 * part + 1], refs[2 * count + part]
        size = mine.shape[0]
        bit = bit_ref[part]
        out[pl.ds(bit * size, size)] = mine[...]
        out[pl.ds((1 - bit) * size, size)] = got[...]


def join(bits, mines, gots):
    operands = [a for pair in zip(mines, gots) for a in pair]
    shapes = [jax.ShapeDtypeStruct((2 * m.shape[0],) + m.shape[1:], BF16) for m in mines]
    size = sum(m.size for m in mines)
    return pl.pallas_call(
        join_kernel,
        grid_spec=pltpu.PrefetchScalarGridSpec(
            num_scalar_prefetch=1,
            grid=(1,),
            in_specs=[whole(a.shape) for a in operands],
            out_specs=[whole(s.shape) for s in shapes],
        ),
        out_shape=shapes,
        compiler_params=params(32),
        cost_estimate=cost(size, 8 * size),
        name="join",
    )(bits, *operands)


def step_bits(orders, step):
    return jnp.stack([bit_of(*order[step]) for order in orders]).astype(jnp.int32)


def send_all(values, orders, step):
    return [swap(value, *order[step]) for value, order in zip(values, orders)]


def tie(*values):
    return lax.optimization_barrier(values)


def sum_all(value, order):
    for axis, bit in order:
        value = value + swap(value, axis, bit)
    return value


def finish_kernel(first, info_ref, a_ref, b_ref, c_ref, *refs):
    down_ref, up_ref, out_ref = refs[-3:]
    main, width = a_ref.shape
    rows = down_ref.shape[0]
    tail = rows - main
    wide = lambda value: value.astype(F32)
    down_ref[:main, :] = wide(a_ref[...])
    down_ref[main:, :] = wide(c_ref[:tail, :])
    for panel in range(rows // width):
        begin, end = panel * width, (panel + 1) * width
        columns = slice(begin, end)
        inner = min(end, main) - begin
        up_ref[:inner, columns] = wide(b_ref[begin : begin + inner, :])
        if inner < width:
            up_ref[inner:, columns] = wide(c_ref[tail : tail + width - inner, :])
    out_ref[...] = wide(c_ref[2 * tail :, :])


def finish(side, parts, hidden, carried=None):
    width = parts[0].shape[1]
    rows = hidden // 2
    shapes = [(hidden, width), (width, hidden), (width, width)]
    specs = [
        pl.BlockSpec((rows, width), lambda i, info: (info[0], 0)),
        pl.BlockSpec((width, rows), lambda i, info: (0, info[0])),
        pl.BlockSpec((width // 2, width), lambda i, info: (info[0], 0)),
    ]
    carried = carried or []
    return pl.pallas_call(
        lambda *refs: finish_kernel(not carried, *refs),
        grid_spec=pltpu.PrefetchScalarGridSpec(
            num_scalar_prefetch=1,
            grid=(1,),
            in_specs=[whole(p.shape) for p in parts] + [pl.BlockSpec(memory_space=pl.ANY)] * len(carried),
            out_specs=specs,
        ),
        out_shape=[jax.ShapeDtypeStruct(s, F32) for s in shapes],
        input_output_aliases={4 + i: i for i in range(len(carried))},
        compiler_params=params(48),
        cost_estimate=cost(3 * rows * width, 12 * rows * width),
        name="finish",
    )(side, *parts, *carried)


def finish_heads_kernel(info_ref, *refs):
    count = (len(refs) - 3) // 2
    for side in range(2):
        base = (info_ref[0] if side == 0 else 1 - info_ref[0]) * count * PAIR
        for pair in range(count):
            source = refs[side * count + pair]
            for part in range(3):
                columns = pl.ds(pl.multiple_of(base + pair * PAIR, PAIR), PAIR)
                refs[2 * count + part][:, columns] = source[:, part * PAIR : (part + 1) * PAIR].astype(F32)


def finish_heads(side, own, there):
    rows = own[0].shape[0]
    width = 2 * len(own) * PAIR
    step = rows // 4
    return pl.pallas_call(
        finish_heads_kernel,
        grid_spec=pltpu.PrefetchScalarGridSpec(
            num_scalar_prefetch=1,
            grid=(rows // step,),
            in_specs=[pl.BlockSpec((step, 3 * PAIR), lambda i, _: (i, 0))] * (2 * len(own)),
            out_specs=[pl.BlockSpec((step, width), lambda i, _: (i, 0))] * 3,
        ),
        out_shape=[jax.ShapeDtypeStruct((rows, width), F32)] * 3,
        compiler_params=params(32),
        cost_estimate=cost(3 * rows * width, 18 * rows * width),
        name="finish_heads",
    )(side, *own, *there)


def local(
    hidden_in,
    seg_lengths,
    query_weight,
    query_bias,
    key_weight,
    value_weight,
    value_bias,
    out_weight,
    out_bias,
    first_gain,
    first_shift,
    up_weight,
    up_bias,
    down_weight,
    down_bias,
    second_gain,
    second_shift,
    cot_out,
    cot_pool,
):
    _, chunk, width = hidden_in.shape
    length = 4 * chunk
    half = width // 2
    hidden_units = up_weight.shape[1]
    dp_order = [("dp", 1 << i) for i in range((lax.axis_size("dp") - 1).bit_length())]
    far, near = ("seq", 2), ("seq", 1)
    high, low = bit_of(*far), bit_of(*near)
    mine = lax.axis_index("seq")
    whole_number = lambda values: jnp.stack([jnp.asarray(v, jnp.int32) for v in values])

    pick = lambda array, i: lax.dynamic_index_in_dim(array, i, 0, keepdims=False)
    own = pick(hidden_in, high)
    came = swap(pick(hidden_in, 1 - high), *far)
    own_there = swap(own, *near)
    came_there = swap(came, *near)
    cot_own = pick(cot_out, high)
    cot_came = swap(pick(cot_out, 1 - high), *far)

    lengths = pick(seg_lengths, high)
    ends = jnp.cumsum(lengths)
    begins = ends - lengths
    sizes = lengths[:NSENT].astype(F32)
    origin = jnp.min(jnp.where(lengths == LONGEST, begins, length))
    inside = lambda t, lo, hi: (t[:, None] >= lo[None, :]) & (t[:, None] < hi[None, :])
    lanes = lambda m: jnp.pad(m, ((0, 0), (0, PAIR - SLOTS)))
    positions = jnp.arange(length, dtype=jnp.int32)
    member = lanes(inside(positions, begins, ends)).astype(BF16)
    turned = (begins - origin) % length
    turned_ends = turned + lengths
    held = lanes(inside(positions, turned, turned_ends))
    query_feature = held.astype(BF16)
    key_feature = jnp.where(held, 0.0, MASKED).astype(BF16)
    block_first = jnp.arange(length // QB, dtype=jnp.int32) * QB
    lowest = jnp.sum(jnp.where(inside(block_first, turned, turned_ends), turned[None, :], 0), axis=1)
    highest = jnp.sum(jnp.where(inside(block_first + QB - 1, turned, turned_ends), turned_ends[None, :], 0), axis=1)
    per = KB // GRAIN
    starts = lowest // GRAIN
    counts = ((highest + GRAIN - 1) // GRAIN - starts + per - 1) // per
    starts = jnp.minimum(starts, length // GRAIN - counts * per)
    ranges = jnp.concatenate([origin[None], starts, counts, low[None]]).astype(jnp.int32)
    turn = whole_number([origin, low])

    take = lambda weight: lax.dynamic_slice_in_dim(weight, low * half, half, 1)
    by_pair = lambda arrays: jnp.concatenate(
        [a[:, g : g + PAIR] for g in range(0, half, PAIR) for a in arrays], axis=1
    )
    vector = lambda bias: lax.dynamic_slice_in_dim(bias, low * half, half, 0)[None, :]
    packed_weight = by_pair([take(query_weight), take(key_weight), take(value_weight)])
    packed_bias = by_pair([vector(query_bias), jnp.zeros((1, half), F32), vector(value_bias)])
    scale = by_pair([jnp.full((1, half), 0.125, F32)] + [jnp.ones((1, half), F32)] * 2)

    places = whole_number([origin, mine, mine ^ 2, mine ^ 1, mine ^ 3])
    rolled_input, packed = project(places, (own, came, own_there, came_there), packed_weight, packed_bias, scale)
    rolled_heads, att_mine, att_send, lse = attend(ranges, packed, query_feature, key_feature)
    att_other = swap(att_send, *near)

    out_mine = lax.dynamic_slice_in_dim(out_weight, low * half, half, 0)
    out_other = lax.dynamic_slice_in_dim(out_weight, (1 - low) * half, half, 0)
    pool_weight = jnp.pad(pick(cot_pool, high) / sizes[:, None], ((0, PAIR - NSENT), (0, 0)))
    pool_upper = pool_weight.astype(BF16)
    pool_weight = jnp.concatenate([pool_upper, (pool_weight - pool_upper.astype(F32)).astype(BF16)], axis=0)
    vectors = jnp.stack([out_bias, first_gain, first_shift, down_bias, second_gain, second_shift])
    token_info = whole_number([high, low, low + 2])
    (
        final, act, branch, normed, pre, attn, d_first, d_att_mine, d_att_send, pool_part, small_part, up_small,
    ) = token_layers(
        token_info, att_mine, att_other, own, came, cot_own, cot_came, member, pool_weight,
        out_mine, out_other, up_weight, down_weight, vectors, up_bias[None, :],
    )
    d_att_other = swap(d_att_send, *near)

    orders = ([far] + dp_order, dp_order[:1] + [far] + dp_order[1:], dp_order[1:] + dp_order[:1] + [far])
    steps = len(orders[0])
    bits = [step_bits(orders, i) for i in range(steps)]
    pieces_of = lambda part: part.reshape((1 << (steps - 1), -1, part.shape[-1]))
    here, over = whole_number([low]), whole_number([1 - low])

    send_down = product(over, act, branch)
    down_there = swap(send_down, *near)
    send_up = product(over, *tie(normed, pre, send_down)[:2])
    up_there = swap(send_up, *near)
    send_out = head_product(*tie(att_other, attn, send_up)[:2])
    out_there = swap(send_out, *near)
    own_out_left, own_attn, _ = tie(att_mine, attn, send_out)
    down_left, down_right, down_there, _ = tie(act, branch, down_there, send_out)
    grad_part_down = product(here, down_left, down_right, down_there)
    up_left, up_right, up_there, _ = tie(normed, pre, up_there, grad_part_down)
    grad_part_up = product(here, up_left, up_right, up_there)
    own_out_left, own_attn, out_there, _ = tie(own_out_left, own_attn, out_there, grad_part_up)
    grad_part_out = head_product(own_out_left, own_attn, out_there)
    stays_and_goes = split(bits[0], grad_part_down, grad_part_up, grad_part_out)
    keeps, sends = [pieces_of(p) for p in stays_and_goes[::2]], [pieces_of(p) for p in stays_and_goes[1::2]]

    class Chain:
        def __init__(self, keeps, sends):
            self.keeps, self.sends, self.step, self.down = keeps, sends, 0, True

        def advance(self, *work):
            gots = send_all(self.sends, orders, self.step)
            gots = tie(*gots, *work)[: len(gots)]
            if self.down:
                self.step += 1
                last = self.step == steps
                out = combine(bits[min(self.step, steps - 1)], self.keeps, gots, last)
                self.keeps, self.sends = out
                if last:
                    self.down, self.step, self.sends = False, steps - 1, self.keeps
            else:
                self.sends = join(bits[self.step], self.sends, gots)
                self.step -= 1

        def before(self, *values):
            out = tie(*values, *self.sends)
            self.sends = list(out[len(values) :])
            return out[: len(values)]

    chain = Chain(keeps, sends)
    d_mine, d_other = chain.before(d_att_mine, d_att_other)
    d_heads, delta = roll_back(turn, d_mine, d_other, rolled_heads)
    d_rest = rest_back(ranges, packed, d_heads, lse, delta, query_feature, key_feature)
    chain.advance(d_rest)
    d_long = []
    for g in range(half // PAIR):
        (heads_in,) = chain.before(d_heads)
        d_long.append(long_back(g, packed, heads_in, lse, delta))
        if g > 0:
            chain.advance(d_long[-1])
    (rest_in,) = chain.before(d_rest)
    *head_parts, d_packed_bias = packed_product(bits[0], rolled_input, d_long, rest_in)
    chain.advance(head_parts[0])
    head_chain = Chain([pieces_of(p) for p in head_parts[::2]], [pieces_of(p) for p in head_parts[1::2]])
    (rest_in,) = head_chain.before(*chain.before(d_rest))
    d_keep, d_send = input_grad(turn, d_long, rest_in, packed_weight)
    d_got = swap(d_send, *near)
    chain.advance(d_keep)
    head_chain.advance(d_keep)
    (d_got,) = head_chain.before(*chain.before(d_got))
    d_inputs = (d_first + d_keep.astype(F32) + d_got.astype(F32)).reshape(2, chunk, width)

    def to_rows(array):
        keep = pick(array, high)
        other = swap(pick(array, 1 - high).astype(BF16), *far).astype(array.dtype)
        return jnp.stack([jnp.where(high == 0, keep, other), jnp.where(high == 0, other, keep)])

    layer_out = to_rows(final.reshape(2, chunk, width))
    grad_hidden = to_rows(d_inputs)

    pool_part = pool_part[:NSENT]
    pool_row = (pool_part + swap(pool_part, *near)) / sizes[:, None]
    pool_far = swap(pool_row, *far)
    pooled = jnp.stack([jnp.where(high == 0, pool_row, pool_far), jnp.where(high == 0, pool_far, pool_row)])

    while chain.step >= 0 or head_chain.step >= 0:
        if chain.step >= 0:
            chain.advance()
        if head_chain.step >= 0:
            head_chain.advance()

    flat = lambda part: part.reshape(-1, part.shape[-1])
    parts = [flat(p) for p in chain.sends]
    there = [swap(p, *near) for p in parts]
    grad_down, grad_up, grad_out = finish(over, there, hidden_units, finish(here, parts, hidden_units))
    parts = [flat(p) for p in head_chain.sends]
    there = [swap(p, *near) for p in parts]
    head_grads = finish_heads(here, parts, there)

    d_packed_bias = d_packed_bias.reshape(half // PAIR, 3, PAIR)
    first_core = low == 0
    spread = lambda part: jnp.where(
        first_core, jnp.concatenate([part, jnp.zeros_like(part)]), jnp.concatenate([jnp.zeros_like(part), part])
    )[None, :]
    small = jnp.concatenate(
        [spread(d_packed_bias[:, 0].reshape(-1)), spread(d_packed_bias[:, 2].reshape(-1)), small_part[:6], up_small.reshape(-1, width)],
        axis=0,
    )
    small = sum_all(small, [near, far] + dp_order)
    return (
        layer_out,
        pooled,
        grad_hidden,
        head_grads[0],
        small[0],
        head_grads[1],
        head_grads[2],
        small[1],
        grad_out,
        small[2],
        small[3],
        small[4],
        grad_up,
        small[8:].reshape(-1),
        grad_down,
        small[5],
        small[6],
        small[7],
    )


def solution(mesh):
    tokens, rows = P("dp", "seq", None), P("dp", None)
    pool = P("dp", None, None)
    return jax.shard_map(
        local,
        mesh=mesh,
        in_specs=(tokens, rows) + (P(),) * 15 + (tokens, pool),
        out_specs=(tokens, pool, tokens) + (P(),) * 15,
        check_vma=False,
    )
```
